32 devices in a mesh: cl: 8 (over z, x), grp: 4 (over y, core).
Axes of the slice: x: 2, y: 2, z: 4, core: 2. Of those that a mesh axis runs over, the one named last changes fastest.
Arguments:
- basis: float32 [16, 4, 64, 128], P(None, 'grp', 'cl'), may hold values from -6 to 6
- near_blocks: bfloat16 [4, 64, 4, 128, 128], P('grp', 'cl'), may hold values from -0.25 to 0.25
- near_list: int32 [4, 64, 4], P('grp', 'cl'), may hold values from 0 to 23
- source_basis: bfloat16 [4, 64, 32, 128], P('grp', 'cl'), may hold values from -0.5 to 0.5
- target_basis: bfloat16 [4, 64, 32, 128], P('grp', 'cl'), may hold values from -1 to 1
- coupling: bfloat16 [4, 128, 1024], P('grp', 'cl'), may hold values from -0.75 to 0.75
- far_target: int32 [4, 128], P('grp'), may hold values from 0 to 63, as said below
- far_source: int32 [4, 128], P('grp', 'cl'), may hold values from 0 to 63, as said below
- far_count: int32 [4, 8], P('grp', 'cl'), may hold values from 8 to 16
Outputs:
- next_vector: float32 [4, 64, 128], P('grp', 'cl')
- hessenberg: float32 [17], replicated
The draws below stay inside these ranges and needn't reach their ends.
Inputs may be any that keep to these rules, and one draw needn't show every extreme that they name: `far_target`: slots are owned in blocks of 16, block d by owner d of the group, whose clusters are d * 8 to (d + 1) * 8 - 1. Except for slot 1 of each owner, a slot's target lies within 16 clusters before or 23 after the owner's first cluster. Slot 1's target is a cluster of owner (d + 4) % 8. `far_source`: except for slot 0 of each owner, a slot's source lies within 80 clusters before or 87 after the owner's first cluster, and where the slot's target obeys the rule above the source differs from it by 16 to 64 clusters. Slot 0's source is a cluster of owner (d + 4) % 8.
All inputs are finite; a program needn't handle non-finite values.
Results may differ from the reference program's by a relative error of at most 0.0039.
Values may be sent and summed in bfloat16 or wider, within the bound.
A program may use at most 64 MiB of HBM per device.

```python
import jax
import jax.numpy as jnp
from jax import lax

P_SIZE = 128
R = 32
CL_DEV = 8
NEAR_K = 4
FAR_DEV = 16
K = 16
CLUSTERS_GRP = 64
PANELS = 32768
N_CL = 8
N_GRP = 4


def far_pairs(key):
    slot_total = N_CL * FAR_DEV
    shape = (N_GRP, slot_total)
    slot_ids = jnp.arange(slot_total, dtype=jnp.int32)
    owner = (slot_ids // FAR_DEV)[None, :]
    local_slot = (slot_ids % FAR_DEV)[None, :]
    key_target = jax.random.fold_in(key, 101)
    key_offset = jax.random.fold_in(key, 202)
    key_sign = jax.random.fold_in(key, 303)
    key_remote = jax.random.fold_in(key, 404)
    target = owner * CL_DEV + jax.random.randint(key_target, shape, -2 * CL_DEV, 3 * CL_DEV, dtype=jnp.int32)
    target = jnp.clip(target, 0, CLUSTERS_GRP - 1)
    reach = min(8 * CL_DEV, CLUSTERS_GRP // 2)
    offset = jax.random.randint(key_offset, shape, 2 * CL_DEV, reach + 1, dtype=jnp.int32)
    direction = jax.random.randint(key_sign, shape, 0, 2, dtype=jnp.int32) * 2 - 1
    upward = target + direction * offset
    source = jnp.where((upward >= 0) & (upward < CLUSTERS_GRP), upward, target - direction * offset)
    opposite = (owner + N_CL // 2) % N_CL * CL_DEV + jax.random.randint(key_remote, shape, 0, CL_DEV, dtype=jnp.int32)
    source = jnp.where(local_slot == 0, opposite, source)
    target = jnp.where(local_slot == 1, opposite, target)
    return (target.astype(jnp.int32), source.astype(jnp.int32))


def draw_far_target(key, part):
    return far_pairs(key)[0]


def draw_far_source(key, part):
    return far_pairs(key)[1]


def plant(result, rng, least, top_value):
    extent = result.shape
    spot = [jax.random.randint(jax.random.fold_in(rng, axis), (), 0, extent[axis]) for axis in range(len(extent))]
    result = result.at[tuple(spot)].set(least)
    longest = extent.index(max(extent))
    spot[longest] = (spot[longest] + 1) % extent[longest]
    return result.at[tuple(spot)].set(top_value)


def block_levels(key, extent, shards, least, top_value):
    def one(position, parts):
        draws = jax.random.uniform(jax.random.fold_in(jax.random.fold_in(key, 6), position), (parts,), jnp.float32, least / len(shards), top_value / len(shards))
        return jnp.repeat(jnp.exp(draws), extent[position] // parts).reshape((-1,) + (1,) * (len(extent) - position - 1))

    gain = one(*shards[0])
    for cut in shards[1:]:
        gain = gain * one(*cut)
    return gain


def gaussian(rng, dims, spread, most, pieces=(), held_as=jnp.bfloat16):
    gain = block_levels(rng, dims, pieces, -0.22, 0.18) if pieces else 1.0
    drawn = jax.random.normal(rng, dims, jnp.float32) * spread * gain
    return jnp.minimum(jnp.maximum(drawn, -most), most).astype(held_as)


def setup_inputs(seed: int = 0) -> dict:
    keys = jax.random.split(jax.random.key(seed), 10)
    return {
        "basis": gaussian(keys[0], (K, N_GRP, CLUSTERS_GRP, P_SIZE), 1.0, 6.0, ((1, 4), (2, 8)), jnp.float32),
        "near_blocks": gaussian(keys[1], (N_GRP, CLUSTERS_GRP, NEAR_K, P_SIZE, P_SIZE), (NEAR_K * P_SIZE) ** -0.5, 0.25, ((0, 4), (1, 8))),
        "near_list": plant(jax.random.randint(keys[2], (N_GRP, CLUSTERS_GRP, NEAR_K), 0, 3 * CL_DEV), jax.random.fold_in(keys[2], 1), 0, (3 * CL_DEV) - 1).astype(jnp.int32),
        "source_basis": gaussian(keys[3], (N_GRP, CLUSTERS_GRP, R, P_SIZE), P_SIZE ** -0.5, 0.5, ((0, 4), (1, 8))),
        "target_basis": gaussian(keys[4], (N_GRP, CLUSTERS_GRP, R, P_SIZE), R ** -0.5, 1.0, ((0, 4), (1, 8))),
        "coupling": gaussian(keys[5], (N_GRP, N_CL * FAR_DEV, R * R), (R * max(1, FAR_DEV // CL_DEV)) ** -0.5, 0.75, ((0, 4), (1, 8))),
        "far_target": draw_far_target(jax.random.fold_in(keys[9], 71), 0),
        "far_source": draw_far_source(jax.random.fold_in(keys[9], 71), 0),
        "far_count": plant(jax.random.randint(keys[8], (N_GRP, N_CL), FAR_DEV // 2, FAR_DEV + 1), jax.random.fold_in(keys[8], 1), FAR_DEV // 2, FAR_DEV).astype(jnp.int32),
    }


def group_image(packed):
    current_bf, current, blocks, near_ids, sbasis, tbasis, couplings, targets, sources, counts = packed
    padded = jnp.pad(current_bf, ((CL_DEV, CL_DEV), (0, 0)))
    window_start = jnp.arange(CLUSTERS_GRP, dtype=jnp.int32) // CL_DEV * CL_DEV
    source_rows = window_start[:, None] + near_ids.astype(jnp.int32)
    gathered = padded[source_rows]
    near_part = jnp.einsum('tkij,tkj->ti', blocks.astype(jnp.float32), gathered.astype(jnp.float32), precision=lax.Precision.HIGHEST)
    expansion = jnp.einsum('srp,sp->sr', sbasis.astype(jnp.float32), current_bf.astype(jnp.float32), precision=lax.Precision.HIGHEST).astype(jnp.bfloat16)
    slot_index = jnp.arange(N_CL * FAR_DEV, dtype=jnp.int32)
    live_mask = (slot_index % FAR_DEV < counts[slot_index // FAR_DEV]).astype(jnp.float32)
    square_blocks = couplings.reshape(N_CL * FAR_DEV, R, R).astype(jnp.float32)
    term = jnp.einsum('bij,bj->bi', square_blocks, expansion[sources].astype(jnp.float32), precision=lax.Precision.HIGHEST) * live_mask[:, None]
    coupled = jnp.zeros((CLUSTERS_GRP, R), jnp.float32).at[targets].add(term).astype(jnp.bfloat16)
    far_part = jnp.einsum('tr,trp->tp', coupled.astype(jnp.float32), tbasis.astype(jnp.float32), precision=lax.Precision.HIGHEST)
    return 0.5 * current + near_part + far_part

def reference(basis, near_blocks, near_list, source_basis, target_basis, coupling, far_target, far_source, far_count):
    current = basis[K - 1]
    current_bf = current.astype(jnp.bfloat16)
    image = lax.map(group_image, (current_bf, current, near_blocks, near_list, source_basis, target_basis, coupling, far_target, far_source, far_count))
    flat_basis = basis.reshape(K, -1)
    flat_image = image.reshape(-1)
    projection = jnp.dot(flat_basis, flat_image, precision=lax.Precision.HIGHEST) / PANELS
    remainder = flat_image - jnp.dot(projection, flat_basis, precision=lax.Precision.HIGHEST)
    new_norm = jnp.sqrt(jnp.sum(remainder * remainder) / PANELS + 1e-06)
    next_vector = (remainder / new_norm).reshape(image.shape)
    return (next_vector, jnp.concatenate([projection, new_norm[None]]))
```

```python
import functools

import jax
import jax.numpy as jnp
from jax import lax
from jax.experimental import pallas as pl
from jax.experimental.pallas import tpu as pltpu
from jax.sharding import PartitionSpec as P

MESH = pl.DeviceIdType.MESH
TARGET_REACH = 2


def target_offsets(n_cl):
    near = {o % n_cl for r in range(1, TARGET_REACH + 1) for o in (r, -r)}
    return sorted((near | {n_cl // 2}) - {0})


def iota(shape, dim):
    return lax.broadcasted_iota(jnp.int32, shape, dim)


def parts3(x):
    hi = x.astype(jnp.bfloat16)
    rest = x - hi.astype(jnp.float32)
    mid = rest.astype(jnp.bfloat16)
    lo = (rest - mid.astype(jnp.float32)).astype(jnp.bfloat16)
    return hi, mid, lo


def dot_t(a, b):
    return lax.dot_general(a, b, (((1,), (1,)), ((), ())), preferred_element_type=jnp.float32)


def dot(a, b):
    return jnp.dot(a, b, preferred_element_type=jnp.float32)


def kernel(
    n_cl,
    n_grp,
    offsets,
    basis_h,
    near_h,
    list_h,
    sb_h,
    tb_h,
    coup_h,
    ft_h,
    fs_h,
    fc_h,
    out_ref,
    hess_ref,
    bv,
    nv,
    lv,
    sbv,
    tbv,
    cv,
    ftv,
    fsv,
    fcv,
    spread,
    gather,
    e_send,
    e_recv,
    halo,
    p_send,
    p_recv,
    ga_send,
    ga_recv,
    gb_send,
    gb_recv,
    r_send,
    r_recv,
    local_sem,
    halo_sem,
    send_sem,
    recv_sem,
):
    f32, bf16 = jnp.float32, jnp.bfloat16
    me, grp = lax.axis_index("cl"), lax.axis_index("grp")
    total = n_cl * n_grp
    flat_me = me * n_grp + grp
    clusters, near_k = lv.shape
    width = bv.shape[1]
    count = bv.shape[0] // clusters
    slots = cv.shape[0]
    ranks = sbv.shape[0] // clusters
    wide = clusters * ranks
    all_cl = n_cl * clusters

    barrier = pltpu.get_barrier_semaphore()

    def far_device(o):
        flat = lax.rem(flat_me + o, total)
        return {"cl": lax.div(flat, n_grp), "grp": lax.rem(flat, n_grp)}

    def greet(o, _):
        pl.semaphore_signal(barrier, inc=1, device_id=far_device(o), device_id_type=MESH)
        return 0

    loads = [
        pltpu.make_async_copy(src, dst, local_sem.at[i])
        for i, (src, dst) in enumerate(
            [
                (basis_h, bv),
                (sb_h, sbv),
                (coup_h, cv),
                (ft_h, ftv),
                (fs_h, fsv),
                (fc_h, fcv),
                (list_h, lv),
                (near_h, nv),
                (tb_h, tbv),
            ]
        )
    ]
    for load in loads:
        load.start()
    lax.fori_loop(1, total, greet, 0)

    loads[0].wait()
    loads[1].wait()
    current = bv[(count - 1) * clusters :, :]
    current_bf = current.astype(bf16)
    own_lane = iota((clusters, wide), 0) == lax.div(iota((clusters, wide), 1), ranks)
    e8 = jnp.where(own_lane, dot_t(current_bf, sbv[...]), 0.0)
    e_send[0] = jnp.sum(e8, axis=0, keepdims=True).astype(bf16).astype(f32)

    pl.semaphore_wait(barrier, total - 1)

    def send(src, dst, which, device):
        return pltpu.make_async_remote_copy(
            src_ref=src,
            dst_ref=dst,
            send_sem=send_sem.at[which],
            recv_sem=recv_sem.at[which],
            device_id=device,
            device_id_type=MESH,
        )

    def send_e(o, _):
        send(e_send, e_recv.at[pl.ds(o - 1, 1)], 0, {"cl": lax.rem(me + o, n_cl)}).start()
        return 0

    lax.fori_loop(1, n_cl, send_e, 0)
    tile = bv.at[pl.ds((count - 1) * clusters, clusters)]
    halos = [
        pltpu.make_async_remote_copy(
            src_ref=tile,
            dst_ref=halo.at[i],
            send_sem=halo_sem.at[i],
            recv_sem=halo_sem.at[2 + i],
            device_id={"cl": lax.rem(me + shift, n_cl)},
            device_id_type=MESH,
        )
        for i, shift in enumerate((1, n_cl - 1))
    ]
    for copy in halos:
        copy.start()

    def fill(ref, test):
        step = 128
        for at in range(0, ref.shape[0], step):
            block = (step, ref.shape[1])
            ref[at : at + step, :] = jnp.where(test(iota(block, 0) + at, iota(block, 1)), 1.0, 0.0).astype(bf16)

    fill(spread, lambda r, c: lax.rem(r, ranks) == lax.rem(c, ranks))
    fill(gather, lambda r, c: lax.div(r, ranks) == lax.rem(c, ranks))

    for load in loads[2:6]:
        load.wait()
    eye = iota((slots, slots), 0) == iota((slots, slots), 1)
    sources = jnp.sum(jnp.where(eye, fsv[...], 0), axis=1, keepdims=True)
    live = iota((slots, 1), 0) < fcv[...]
    behind = lax.rem(me - lax.div(sources, clusters) + n_cl, n_cl)
    picked_row = jnp.where(live, behind * clusters + lax.rem(sources, clusters), -1)
    one_hot = jnp.where(iota((slots, all_cl), 1) == picked_row, 1.0, 0.0).astype(bf16)
    slot_shape = (slots, ftv.shape[1])
    mine = iota(slot_shape, 1) == iota(slot_shape, 0) + me * slots
    targets = jnp.sum(jnp.where(mine, ftv[...], 0), axis=1, keepdims=True)
    target_dev = lax.div(targets, clusters)
    target_lane = lax.rem(targets, clusters) == lax.div(iota((slots, wide), 1), ranks)

    gram = jnp.zeros((count, count), f32)
    for t in range(clusters):
        rows = bv[pl.ds(t, count, stride=clusters), :]
        gram += lax.dot_general(
            rows, rows, (((1,), (1,)), ((), ())), precision=lax.Precision.HIGHEST, preferred_element_type=f32
        )
    flat_gram = count * count
    widen = jnp.where(
        iota((count, flat_gram), 0) == lax.rem(iota((count, flat_gram), 1), count), 1.0, 0.0
    ).astype(bf16)
    gram_lane = iota((count, flat_gram), 0) == lax.div(iota((count, flat_gram), 1), count)
    gram_wide = sum(dot(part, widen) for part in parts3(gram))
    ga_send[0] = jnp.sum(jnp.where(gram_lane, gram_wide, 0.0), axis=0, keepdims=True)

    def send_ga(o, _):
        send(ga_send, ga_recv.at[pl.ds(o - 1, 1)], 1, {"cl": lax.rem(me + o, n_cl)}).start()
        return 0

    lax.fori_loop(1, n_cl, send_ga, 0)

    def arrived(ref, which):
        pltpu.make_async_copy(ref, ref, recv_sem.at[which]).wait()

    def left(ref, which):
        pltpu.make_async_copy(ref, ref, send_sem.at[which]).wait()

    arrived(e_recv, 0)
    rows = jnp.concatenate([e_send[...], e_recv[...]], axis=0)
    rows = jnp.where(own_lane[None], jnp.broadcast_to(rows, (n_cl, clusters, wide)), 0.0)
    picked = dot(one_hot, rows.reshape(all_cl, wide).astype(bf16)).astype(bf16)
    product = dot(picked, spread[...]) * cv[...].astype(f32)
    high = product.astype(bf16)
    low = (product - high.astype(f32)).astype(bf16)
    term = dot(high, gather[...]) + dot(low, gather[...])
    term = jnp.where(target_lane, term, 0.0)

    def partial_for(device):
        return jnp.sum(jnp.where(target_dev == device, term, 0.0), axis=0, keepdims=True)

    for i, o in enumerate(offsets):
        p_send[i] = partial_for(lax.rem(me + o, n_cl))
    for i, o in enumerate(offsets):
        send(p_send.at[i], p_recv.at[i], 2, {"cl": lax.rem(me + o, n_cl)}).start()
    own_partial = partial_for(me)

    for i in range(2):
        halos[i].wait_recv()
    loads[6].wait()
    before = jnp.where(me > 0, halo[0], 0.0)
    after = jnp.where(me < n_cl - 1, halo[1], 0.0)
    window = jnp.concatenate([before, current, after], axis=0).astype(bf16)
    reach = window.shape[0]
    listed = lv[...]
    gathered = jnp.concatenate(
        [
            dot(
                jnp.where(iota((clusters, reach), 1) == listed[:, k : k + 1], 1.0, 0.0).astype(bf16), window
            ).astype(bf16)
            for k in range(near_k)
        ],
        axis=1,
    )
    loads[7].wait()
    image = 0.5 * current
    pair = 2
    row_id = iota((clusters, width), 0)
    for t in range(0, clusters, pair):
        blocks = jnp.concatenate(
            [
                jnp.concatenate([nv[(t + u) * near_k + k] for k in range(near_k)], axis=1)
                for u in range(pair)
            ],
            axis=0,
        )
        result = dot_t(gathered, blocks)
        for u in range(pair):
            image += jnp.where(row_id == t + u, result[:, u * width : (u + 1) * width], 0.0)

    arrived(ga_recv, 1)
    group_gram = ga_send[0] + jnp.sum(ga_recv[...], axis=0)
    gb_send[0] = group_gram

    def send_gb(o, _):
        send(gb_send, gb_recv.at[pl.ds(o - 1, 1)], 3, {"grp": lax.rem(grp + o, n_grp)}).start()
        return 0

    lax.fori_loop(1, n_grp, send_gb, 0)

    loads[8].wait()
    arrived(p_recv, 2)
    coupled = own_partial + jnp.sum(p_recv[...], axis=0)
    coupled = jnp.where(own_lane, jnp.broadcast_to(coupled, (clusters, wide)), 0.0).astype(bf16)
    image += dot(coupled, tbv[...])

    basis3 = bv[...].reshape(count, clusters, width)
    sums = jnp.sum(basis3 * image[None], axis=1)
    squares = jnp.sum(image * image, axis=0, keepdims=True)
    tail = jnp.where(iota((8, width), 0) == 0, squares, 0.0)
    stacked = jnp.concatenate([sums, tail, jnp.zeros((width - count - 8, width), f32)], axis=0)
    ones = jnp.ones((8, width), bf16)
    row = sum(dot_t(ones, part) for part in parts3(stacked))[0:1]
    r_send[0] = row

    def send_r(o, _):
        send(r_send, r_recv.at[pl.ds(o - 1, 1)], 4, far_device(o)).start()
        return 0

    lax.fori_loop(1, total, send_r, 0)

    arrived(gb_recv, 3)
    whole_gram = gb_send[0] + jnp.sum(gb_recv[...], axis=0)
    narrow = jnp.where(
        lax.rem(iota((flat_gram, width), 0), count) == iota((flat_gram, width), 1), 1.0, 0.0
    ).astype(bf16)
    gram_rows = jnp.where(gram_lane, jnp.broadcast_to(whole_gram, (count, flat_gram)), 0.0)
    gram_full = sum(dot(part, narrow) for part in parts3(gram_rows))

    arrived(r_recv, 4)
    inverse = 1.0 / float(total * clusters * width)
    mean = (r_send[0] + jnp.sum(r_recv[...], axis=0)) * inverse
    diagonal = iota((count, width), 0) == iota((count, width), 1)
    projection = jnp.sum(jnp.where(diagonal, mean, 0.0), axis=1, keepdims=True)
    applied = jnp.sum(gram_full * mean, axis=1, keepdims=True) * inverse
    lane = iota((1, width), 1)
    image_mean = jnp.sum(jnp.where(lane == count, mean, 0.0), axis=1, keepdims=True)
    change = jnp.sum(projection * (applied - 2.0 * projection), axis=0, keepdims=True)
    norm = jnp.sqrt(image_mean + change + 1e-06)
    spread_p = jnp.broadcast_to(projection, (count, width))
    remainder = image - jnp.sum(basis3 * spread_p[:, None, :], axis=0)
    out_ref[...] = remainder * (1.0 / norm)
    hess_ref[...] = jnp.where(lane == count, norm, mean)[:, : count + 1]

    for i in range(2):
        halos[i].wait_send()
    left(e_recv, 0)
    left(ga_recv, 1)
    left(p_recv, 2)
    left(gb_recv, 3)
    left(r_recv, 4)


def on_device(n_cl, n_grp, basis, near_blocks, near_list, source_basis, target_basis, coupling, far_target, far_source, far_count):
    count, _, clusters, width = basis.shape
    near_k = near_blocks.shape[2]
    ranks = source_basis.shape[2]
    slots = coupling.shape[1]
    wide = clusters * ranks
    square = ranks * ranks
    total = n_cl * n_grp
    offsets = target_offsets(n_cl)
    args = (
        basis.reshape(count * clusters, width),
        near_blocks.reshape(clusters * near_k, width, width),
        near_list.reshape(clusters, near_k),
        source_basis.reshape(wide, width),
        target_basis.reshape(wide, width),
        coupling.reshape(slots, square),
        far_target,
        far_source,
        far_count,
    )
    f32, bf16 = jnp.float32, jnp.bfloat16
    order = (0, 1, 2, 3, 4, 5, 6, 7, 8)
    next_vector, hessenberg = pl.pallas_call(
        functools.partial(kernel, n_cl, n_grp, offsets),
        out_shape=(
            jax.ShapeDtypeStruct((clusters, width), f32),
            jax.ShapeDtypeStruct((1, count + 1), f32),
        ),
        in_specs=[pl.BlockSpec(memory_space=pl.ANY)] * len(args),
        out_specs=(pl.BlockSpec(memory_space=pltpu.VMEM), pl.BlockSpec(memory_space=pltpu.VMEM)),
        scratch_shapes=[pltpu.VMEM(args[i].shape, args[i].dtype) for i in order]
        + [
            pltpu.VMEM((wide, square), bf16),
            pltpu.VMEM((square, wide), bf16),
            pltpu.VMEM((1, 1, wide), f32),
            pltpu.VMEM((n_cl - 1, 1, wide), f32),
            pltpu.VMEM((2, clusters, width), f32),
            pltpu.VMEM((len(offsets), 1, wide), f32),
            pltpu.VMEM((len(offsets), 1, wide), f32),
            pltpu.VMEM((1, 1, count * count), f32),
            pltpu.VMEM((n_cl - 1, 1, count * count), f32),
            pltpu.VMEM((1, 1, count * count), f32),
            pltpu.VMEM((n_grp - 1, 1, count * count), f32),
            pltpu.VMEM((1, 1, width), f32),
            pltpu.VMEM((total - 1, 1, width), f32),
            pltpu.SemaphoreType.DMA((9,)),
            pltpu.SemaphoreType.DMA((4,)),
            pltpu.SemaphoreType.DMA((5,)),
            pltpu.SemaphoreType.DMA((5,)),
        ],
        compiler_params=pltpu.CompilerParams(collective_id=0, has_side_effects=True),
        name="arnoldi_step",
    )(*args)
    return next_vector.reshape(1, clusters, width), hessenberg.reshape(count + 1)


def solution(mesh):
    placed = (
        P(None, "grp", "cl", None),
        P("grp", "cl", None, None, None),
        P("grp", "cl", None),
        P("grp", "cl", None, None),
        P("grp", "cl", None, None),
        P("grp", "cl", None),
        P("grp", None),
        P("grp", "cl"),
        P("grp", "cl"),
    )
    return jax.shard_map(
        functools.partial(on_device, mesh.shape["cl"], mesh.shape["grp"]),
        mesh=mesh,
        in_specs=placed,
        out_specs=(P("grp", "cl", None), P()),
        check_vma=False,
    )
```

```python
import functools

import jax
import jax.numpy as jnp
from jax import lax
from jax.experimental import pallas as pl
from jax.experimental.pallas import tpu as pltpu
from jax.sharding import PartitionSpec as P

MESH = pl.DeviceIdType.MESH
TARGET_REACH = 2


def target_offsets(n_cl):
    near = {o % n_cl for r in range(1, TARGET_REACH + 1) for o in (r, -r)}
    return sorted((near | {n_cl // 2}) - {0})


def iota(shape, dim):
    return lax.broadcasted_iota(jnp.int32, shape, dim)


def power_of_two(n):
    return n & (n - 1) == 0


def quot(x, n):
    return lax.shift_right_logical(x, n.bit_length() - 1) if power_of_two(n) else lax.div(x, n)


def rest(x, n):
    return x & (n - 1) if power_of_two(n) else lax.rem(x, n)


def partner(me, o, n):
    return me ^ o if power_of_two(n) else lax.rem(me + o, n)


def place_of(me, device, n):
    return me ^ device if power_of_two(n) else lax.rem(me - device + n, n)


def for_others(n, body):
    if n <= 64:
        for o in range(1, n):
            body(o)
    else:
        pl.loop(1, n)(body)


def parts3(x):
    hi = x.astype(jnp.bfloat16)
    rest = x - hi.astype(jnp.float32)
    mid = rest.astype(jnp.bfloat16)
    lo = (rest - mid.astype(jnp.float32)).astype(jnp.bfloat16)
    return hi, mid, lo


def dot_t(a, b):
    return lax.dot_general(a, b, (((1,), (1,)), ((), ())), preferred_element_type=jnp.float32)


def dot(a, b):
    return jnp.dot(a, b, preferred_element_type=jnp.float32)


def kernel(
    n_cl,
    n_grp,
    offsets,
    basis_h,
    near_h,
    list_h,
    sb_h,
    tb_h,
    coup_h,
    ft_h,
    fs_h,
    fc_h,
    out_ref,
    hess_ref,
    bv,
    nv,
    lv,
    sbv,
    tbv,
    cv,
    ftv,
    fsv,
    fcv,
    spread,
    gather,
    e_send,
    e_recv,
    halo,
    p_send,
    p_recv,
    ga_send,
    ga_recv,
    gb_send,
    gb_recv,
    r_send,
    r_recv,
    local_sem,
    halo_sem,
    send_sem,
    recv_sem,
):
    f32, bf16 = jnp.float32, jnp.bfloat16
    me, grp = lax.axis_index("cl"), lax.axis_index("grp")
    total = n_cl * n_grp
    flat_me = me * n_grp + grp
    near_k, clusters = lv.shape
    width = bv.shape[1]
    count = bv.shape[0] // clusters
    slots = cv.shape[0]
    ranks = sbv.shape[0] // clusters
    wide = clusters * ranks
    all_cl = n_cl * clusters

    barrier = pltpu.get_barrier_semaphore()

    def far_device(o):
        flat = partner(flat_me, o, total)
        return {"cl": quot(flat, n_grp), "grp": rest(flat, n_grp)}

    def greet(o):
        pl.semaphore_signal(barrier, inc=1, device_id=far_device(o), device_id_type=MESH)

    for_others(total, greet)
    loads = [
        pltpu.make_async_copy(src, dst, local_sem.at[i])
        for i, (src, dst) in enumerate(
            [
                (basis_h, bv),
                (sb_h, sbv),
                (coup_h, cv),
                (ft_h, ftv),
                (fs_h, fsv),
                (fc_h, fcv),
                (list_h, lv),
                (near_h, nv),
                (tb_h, tbv),
            ]
        )
    ]
    for load in loads:
        load.start()

    loads[0].wait()
    loads[1].wait()
    current = bv[(count - 1) * clusters :, :]
    current_bf = current.astype(bf16)
    own_lane = iota((clusters, wide), 0) == quot(iota((clusters, wide), 1), ranks)
    e8 = jnp.where(own_lane, dot_t(current_bf, sbv[...]), 0.0)
    e_send[0] = jnp.sum(e8, axis=0, keepdims=True).astype(bf16).astype(f32)

    pl.semaphore_wait(barrier, total - 1)

    def send(src, dst, which, device):
        return pltpu.make_async_remote_copy(
            src_ref=src,
            dst_ref=dst,
            send_sem=send_sem.at[which],
            recv_sem=recv_sem.at[which],
            device_id=device,
            device_id_type=MESH,
        )

    def send_e(o):
        send(e_send, e_recv.at[pl.ds(o - 1, 1)], 0, {"cl": partner(me, o, n_cl)}).start()

    for_others(n_cl, send_e)
    tile = bv.at[pl.ds((count - 1) * clusters, clusters)]
    halos = [
        pltpu.make_async_remote_copy(
            src_ref=tile,
            dst_ref=halo.at[i],
            send_sem=halo_sem.at[i],
            recv_sem=halo_sem.at[2 + i],
            device_id={"cl": rest(me + shift, n_cl)},
            device_id_type=MESH,
        )
        for i, shift in enumerate((1, n_cl - 1))
    ]
    for copy in halos:
        copy.start()

    repeat = jnp.where(
        iota((ranks, ranks * ranks), 0) == rest(iota((ranks, ranks * ranks), 1), ranks), 1.0, 0.0
    ).astype(bf16)
    for at in range(0, wide, ranks):
        spread[at : at + ranks, :] = repeat
    lane_rank = rest(iota((ranks, wide), 1), ranks)
    for r in range(ranks):
        gather[r * ranks : (r + 1) * ranks, :] = jnp.where(lane_rank == r, 1.0, 0.0).astype(bf16)

    for load in loads[2:6]:
        load.wait()
    eye = iota((slots, slots), 0) == iota((slots, slots), 1)
    sources = jnp.sum(jnp.where(eye, fsv[...], 0), axis=1, keepdims=True)
    live = iota((slots, 1), 0) < fcv[...]
    behind = place_of(me, quot(sources, clusters), n_cl)
    picked_row = jnp.where(live, behind * clusters + rest(sources, clusters), -1)
    one_hot = jnp.where(iota((slots, all_cl), 1) == picked_row, 1.0, 0.0).astype(bf16)
    slot_shape = (slots, ftv.shape[1])
    mine = iota(slot_shape, 1) == iota(slot_shape, 0) + me * slots
    targets = jnp.sum(jnp.where(mine, ftv[...], 0), axis=1, keepdims=True)
    target_dev = quot(targets, clusters)
    target_lane = rest(targets, clusters) == quot(iota((slots, wide), 1), ranks)

    gram = jnp.zeros((count, count), f32)
    for t in range(clusters):
        rows = bv[pl.ds(t, count, stride=clusters), :]
        gram += lax.dot_general(
            rows, rows, (((1,), (1,)), ((), ())), precision=lax.Precision.HIGHEST, preferred_element_type=f32
        )
    flat_gram = count * count
    widen = jnp.where(
        iota((count, flat_gram), 0) == rest(iota((count, flat_gram), 1), count), 1.0, 0.0
    ).astype(bf16)
    gram_lane = iota((count, flat_gram), 0) == quot(iota((count, flat_gram), 1), count)
    gram_wide = sum(dot(part, widen) for part in parts3(gram))
    ga_send[0] = jnp.sum(jnp.where(gram_lane, gram_wide, 0.0), axis=0, keepdims=True)

    def send_ga(o):
        send(ga_send, ga_recv.at[pl.ds(o - 1, 1)], 1, {"cl": partner(me, o, n_cl)}).start()

    for_others(n_cl, send_ga)

    def arrived(ref, which):
        pltpu.make_async_copy(ref, ref, recv_sem.at[which]).wait()

    def left(ref, which):
        pltpu.make_async_copy(ref, ref, send_sem.at[which]).wait()

    arrived(e_recv, 0)
    rows = jnp.concatenate([e_send[...], e_recv[...]], axis=0)
    rows = jnp.where(own_lane[None], jnp.broadcast_to(rows, (n_cl, clusters, wide)), 0.0)
    picked = dot(one_hot, rows.reshape(all_cl, wide).astype(bf16)).astype(bf16)
    product = dot(picked, spread[...]) * cv[...].astype(f32)
    high = product.astype(bf16)
    low = (product - high.astype(f32)).astype(bf16)
    term = dot(high, gather[...]) + dot(low, gather[...])
    term = jnp.where(target_lane, term, 0.0)

    def partial_for(device):
        return jnp.sum(jnp.where(target_dev == device, term, 0.0), axis=0, keepdims=True)

    for i, o in enumerate(offsets):
        p_send[i] = partial_for(rest(me + o, n_cl))
    for i, o in enumerate(offsets):
        send(p_send.at[i], p_recv.at[i], 2, {"cl": rest(me + o, n_cl)}).start()
    own_partial = partial_for(me)

    for i in range(2):
        halos[i].wait_recv()
    loads[6].wait()
    before = jnp.where(me > 0, halo[0], 0.0)
    after = jnp.where(me < n_cl - 1, halo[1], 0.0)
    window = jnp.concatenate([before, current, after], axis=0).astype(bf16)
    reach = window.shape[0]
    turn = iota((clusters, clusters), 0) == iota((clusters, clusters), 1)
    listed = [
        jnp.sum(jnp.where(turn, lv[k : k + 1, :], 0), axis=1, keepdims=True) for k in range(near_k)
    ]
    gathered = jnp.concatenate(
        [
            dot(
                jnp.where(iota((clusters, reach), 1) == listed[k], 1.0, 0.0).astype(bf16), window
            ).astype(bf16)
            for k in range(near_k)
        ],
        axis=1,
    )
    loads[7].wait()
    image = 0.5 * current
    pair = 2
    row_id = iota((clusters, width), 0)
    for t in range(0, clusters, pair):
        blocks = jnp.concatenate(
            [
                jnp.concatenate([nv[(t + u) * near_k + k] for k in range(near_k)], axis=1)
                for u in range(pair)
            ],
            axis=0,
        )
        result = dot_t(gathered, blocks)
        for u in range(pair):
            image += jnp.where(row_id == t + u, result[:, u * width : (u + 1) * width], 0.0)

    arrived(ga_recv, 1)
    group_gram = ga_send[0] + jnp.sum(ga_recv[...], axis=0)
    gb_send[0] = group_gram

    def send_gb(o):
        send(gb_send, gb_recv.at[pl.ds(o - 1, 1)], 3, {"grp": partner(grp, o, n_grp)}).start()

    for_others(n_grp, send_gb)

    loads[8].wait()
    arrived(p_recv, 2)
    coupled = own_partial + jnp.sum(p_recv[...], axis=0)
    coupled = jnp.where(own_lane, jnp.broadcast_to(coupled, (clusters, wide)), 0.0).astype(bf16)
    image += dot(coupled, tbv[...])

    basis3 = bv[...].reshape(count, clusters, width)
    sums = jnp.sum(basis3 * image[None], axis=1)
    squares = jnp.sum(image * image, axis=0, keepdims=True)
    tail = jnp.where(iota((8, width), 0) == 0, squares, 0.0)
    stacked = jnp.concatenate([sums, tail, jnp.zeros((width - count - 8, width), f32)], axis=0)
    ones = jnp.ones((8, width), bf16)
    row = sum(dot_t(ones, part) for part in parts3(stacked))[0:1]
    r_send[0] = row

    def send_r(o):
        send(r_send, r_recv.at[pl.ds(o - 1, 1)], 4, far_device(o)).start()

    for_others(total, send_r)

    arrived(gb_recv, 3)
    whole_gram = gb_send[0] + jnp.sum(gb_recv[...], axis=0)
    narrow = jnp.where(
        rest(iota((flat_gram, width), 0), count) == iota((flat_gram, width), 1), 1.0, 0.0
    ).astype(bf16)
    gram_rows = jnp.where(gram_lane, jnp.broadcast_to(whole_gram, (count, flat_gram)), 0.0)
    gram_full = sum(dot(part, narrow) for part in parts3(gram_rows))

    arrived(r_recv, 4)
    inverse = 1.0 / float(total * clusters * width)
    mean = (r_send[0] + jnp.sum(r_recv[...], axis=0)) * inverse
    diagonal = iota((count, width), 0) == iota((count, width), 1)
    projection = jnp.sum(jnp.where(diagonal, mean, 0.0), axis=1, keepdims=True)
    applied = jnp.sum(gram_full * mean, axis=1, keepdims=True) * inverse
    lane = iota((1, width), 1)
    image_mean = jnp.sum(jnp.where(lane == count, mean, 0.0), axis=1, keepdims=True)
    change = jnp.sum(projection * (applied - 2.0 * projection), axis=0, keepdims=True)
    norm = jnp.sqrt(image_mean + change + 1e-06)
    spread_p = jnp.broadcast_to(projection, (count, width))
    remainder = image - jnp.sum(basis3 * spread_p[:, None, :], axis=0)
    out_ref[...] = remainder * (1.0 / norm)
    hess_ref[...] = jnp.where(lane == count, norm, mean)[:, : count + 1]

    for i in range(2):
        halos[i].wait_send()
    left(e_recv, 0)
    left(ga_recv, 1)
    left(p_recv, 2)
    left(gb_recv, 3)
    left(r_recv, 4)


def hand_out(vector, column, vector_h, column_h, sem):
    copies = [
        pltpu.make_async_copy(vector, vector_h, sem.at[0]),
        pltpu.make_async_copy(column, column_h, sem.at[1]),
    ]
    for copy in copies:
        copy.start()
    for copy in copies:
        copy.wait()


def on_device(n_cl, n_grp, basis, near_blocks, near_list, source_basis, target_basis, coupling, far_target, far_source, far_count):
    count, _, clusters, width = basis.shape
    near_k = near_blocks.shape[2]
    ranks = source_basis.shape[2]
    slots = coupling.shape[1]
    wide = clusters * ranks
    square = ranks * ranks
    total = n_cl * n_grp
    offsets = target_offsets(n_cl)
    args = (
        basis.reshape(count * clusters, width),
        near_blocks.reshape(clusters * near_k, width, width),
        near_list.reshape(clusters, near_k).T,
        source_basis.reshape(wide, width),
        target_basis.reshape(wide, width),
        coupling.reshape(slots, square),
        far_target,
        far_source,
        far_count,
    )
    f32, bf16 = jnp.float32, jnp.bfloat16
    order = (0, 1, 2, 3, 4, 5, 6, 7, 8)
    next_vector, hessenberg = pl.pallas_call(
        functools.partial(kernel, n_cl, n_grp, offsets),
        out_shape=(
            pltpu.VMEM((clusters, width), f32),
            pltpu.VMEM((1, count + 1), f32),
        ),
        in_specs=[pl.BlockSpec(memory_space=pl.ANY)] * len(args),
        out_specs=(pl.BlockSpec(memory_space=pltpu.VMEM), pl.BlockSpec(memory_space=pltpu.VMEM)),
        scratch_shapes=[pltpu.VMEM(args[i].shape, args[i].dtype) for i in order]
        + [
            pltpu.VMEM((wide, square), bf16),
            pltpu.VMEM((square, wide), bf16),
            pltpu.VMEM((1, 1, wide), f32),
            pltpu.VMEM((n_cl - 1, 1, wide), f32),
            pltpu.VMEM((2, clusters, width), f32),
            pltpu.VMEM((len(offsets), 1, wide), f32),
            pltpu.VMEM((len(offsets), 1, wide), f32),
            pltpu.VMEM((1, 1, count * count), f32),
            pltpu.VMEM((n_cl - 1, 1, count * count), f32),
            pltpu.VMEM((1, 1, count * count), f32),
            pltpu.VMEM((n_grp - 1, 1, count * count), f32),
            pltpu.VMEM((1, 1, width), f32),
            pltpu.VMEM((total - 1, 1, width), f32),
            pltpu.SemaphoreType.DMA((9,)),
            pltpu.SemaphoreType.DMA((4,)),
            pltpu.SemaphoreType.DMA((5,)),
            pltpu.SemaphoreType.DMA((5,)),
        ],
        compiler_params=pltpu.CompilerParams(collective_id=0, has_side_effects=True),
        name="arnoldi_step",
    )(*args)
    next_vector = pltpu.with_memory_space_constraint(next_vector, pltpu.VMEM)
    hessenberg = pltpu.with_memory_space_constraint(hessenberg, pltpu.VMEM)
    next_vector, hessenberg = pl.pallas_call(
        hand_out,
        out_shape=(
            jax.ShapeDtypeStruct((clusters, width), f32),
            jax.ShapeDtypeStruct((1, count + 1), f32),
        ),
        in_specs=[pl.BlockSpec(memory_space=pltpu.VMEM)] * 2,
        out_specs=(pl.BlockSpec(memory_space=pl.ANY), pl.BlockSpec(memory_space=pl.ANY)),
        scratch_shapes=[pltpu.SemaphoreType.DMA((2,))],
        name="hand_out",
    )(next_vector, hessenberg)
    return next_vector.reshape(1, clusters, width), hessenberg.reshape(count + 1)


def solution(mesh):
    placed = (
        P(None, "grp", "cl", None),
        P("grp", "cl", None, None, None),
        P("grp", "cl", None),
        P("grp", "cl", None, None),
        P("grp", "cl", None, None),
        P("grp", "cl", None),
        P("grp", None),
        P("grp", "cl"),
        P("grp", "cl"),
    )
    return jax.shard_map(
        functools.partial(on_device, mesh.shape["cl"], mesh.shape["grp"]),
        mesh=mesh,
        in_specs=placed,
        out_specs=(P("grp", "cl", None), P()),
        check_vma=False,
    )
```

```python
import functools

import jax
import jax.numpy as jnp
from jax import lax
from jax.experimental import pallas as pl
from jax.experimental.pallas import tpu as pltpu
from jax.sharding import PartitionSpec as P

MESH = pl.DeviceIdType.MESH
TARGET_REACH = 2


def target_offsets(n_cl):
    near = {o % n_cl for r in range(1, TARGET_REACH + 1) for o in (r, -r)}
    return sorted((near | {n_cl // 2}) - {0})


def iota(shape, dim):
    return lax.broadcasted_iota(jnp.int32, shape, dim)


def power_of_two(n):
    return n & (n - 1) == 0


def quot(x, n):
    return lax.shift_right_logical(x, n.bit_length() - 1) if power_of_two(n) else lax.div(x, n)


def rest(x, n):
    return x & (n - 1) if power_of_two(n) else lax.rem(x, n)


def partner(me, o, n):
    return me ^ o if power_of_two(n) else lax.rem(me + o, n)


def place_of(me, device, n):
    return me ^ device if power_of_two(n) else lax.rem(me - device + n, n)


def for_others(n, body):
    if n <= 64:
        for o in reversed(range(1, n)):
            body(o)
    else:
        pl.loop(1, n)(body)


def parts3(x):
    hi = x.astype(jnp.bfloat16)
    rest = x - hi.astype(jnp.float32)
    mid = rest.astype(jnp.bfloat16)
    lo = (rest - mid.astype(jnp.float32)).astype(jnp.bfloat16)
    return hi, mid, lo


def dot_t(a, b):
    return lax.dot_general(a, b, (((1,), (1,)), ((), ())), preferred_element_type=jnp.float32)


def dot(a, b):
    return jnp.dot(a, b, preferred_element_type=jnp.float32)


def kernel(
    n_cl,
    n_grp,
    offsets,
    basis_h,
    near_h,
    list_h,
    sb_h,
    tb_h,
    coup_h,
    ft_h,
    fs_h,
    fc_h,
    out_ref,
    hess_ref,
    bv,
    nv,
    lv,
    sbv,
    tbv,
    cv,
    ftv,
    fsv,
    fcv,
    spread,
    gather,
    e_send,
    e_recv,
    halo,
    p_send,
    p_recv,
    ga_send,
    ga_recv,
    gb_send,
    gb_recv,
    r_send,
    r_recv,
    local_sem,
    halo_sem,
    send_sem,
    recv_sem,
):
    f32, bf16 = jnp.float32, jnp.bfloat16
    me, grp = lax.axis_index("cl"), lax.axis_index("grp")
    total = n_cl * n_grp
    flat_me = me * n_grp + grp
    near_k, clusters = lv.shape
    width = bv.shape[1]
    count = bv.shape[0] // clusters
    slots = cv.shape[0]
    ranks = sbv.shape[0] // clusters
    wide = clusters * ranks
    all_cl = n_cl * clusters

    barrier = pltpu.get_barrier_semaphore()

    def far_device(o):
        flat = partner(flat_me, o, total)
        return {"cl": quot(flat, n_grp), "grp": rest(flat, n_grp)}

    def greet(axis, mine, n):
        def one(o):
            device = {axis: partner(mine, o, n)}
            pl.semaphore_signal(barrier, inc=1, device_id=device, device_id_type=MESH)

        for_others(n, one)

    greet("cl", me, n_cl)
    greet("grp", grp, n_grp)
    loads = [
        pltpu.make_async_copy(src, dst, local_sem.at[i])
        for i, (src, dst) in enumerate(
            [
                (basis_h, bv),
                (sb_h, sbv),
                (coup_h, cv),
                (ft_h, ftv),
                (fs_h, fsv),
                (fc_h, fcv),
                (list_h, lv),
                (near_h, nv),
                (tb_h, tbv),
            ]
        )
    ]
    for load in loads:
        load.start()

    loads[0].wait()
    loads[1].wait()
    current = bv[(count - 1) * clusters :, :]
    current_bf = current.astype(bf16)
    own_lane = iota((clusters, wide), 0) == quot(iota((clusters, wide), 1), ranks)
    e8 = jnp.where(own_lane, dot_t(current_bf, sbv[...]), 0.0)
    e_send[0] = jnp.sum(e8, axis=0, keepdims=True).astype(bf16).astype(f32)

    repeat = jnp.where(
        iota((ranks, ranks * ranks), 0) == rest(iota((ranks, ranks * ranks), 1), ranks), 1.0, 0.0
    ).astype(bf16)
    for at in range(0, wide, ranks):
        spread[at : at + ranks, :] = repeat
    lane_rank = rest(iota((ranks, wide), 1), ranks)
    for r in range(ranks):
        gather[r * ranks : (r + 1) * ranks, :] = jnp.where(lane_rank == r, 1.0, 0.0).astype(bf16)

    for load in loads[2:6]:
        load.wait()
    eye = iota((slots, slots), 0) == iota((slots, slots), 1)
    sources = jnp.sum(jnp.where(eye, fsv[...], 0), axis=1, keepdims=True)
    live = iota((slots, 1), 0) < fcv[...]
    behind = place_of(me, quot(sources, clusters), n_cl)
    picked_row = jnp.where(live, behind * clusters + rest(sources, clusters), -1)
    one_hot = jnp.where(iota((slots, all_cl), 1) == picked_row, 1.0, 0.0).astype(bf16)
    slot_shape = (slots, ftv.shape[1])
    mine = iota(slot_shape, 1) == iota(slot_shape, 0) + me * slots
    targets = jnp.sum(jnp.where(mine, ftv[...], 0), axis=1, keepdims=True)
    target_dev = quot(targets, clusters)
    target_lane = rest(targets, clusters) == quot(iota((slots, wide), 1), ranks)

    gram = jnp.zeros((count, count), f32)
    for t in range(clusters):
        rows = bv[pl.ds(t, count, stride=clusters), :]
        gram += lax.dot_general(
            rows, rows, (((1,), (1,)), ((), ())), precision=lax.Precision.HIGHEST, preferred_element_type=f32
        )
    flat_gram = count * count
    widen = jnp.where(
        iota((count, flat_gram), 0) == rest(iota((count, flat_gram), 1), count), 1.0, 0.0
    ).astype(bf16)
    gram_lane = iota((count, flat_gram), 0) == quot(iota((count, flat_gram), 1), count)
    gram_wide = sum(dot(part, widen) for part in parts3(gram))
    ga_send[0] = jnp.sum(jnp.where(gram_lane, gram_wide, 0.0), axis=0, keepdims=True)

    pl.semaphore_wait(barrier, n_cl + n_grp - 2)

    def send(src, dst, which, device):
        return pltpu.make_async_remote_copy(
            src_ref=src,
            dst_ref=dst,
            send_sem=send_sem.at[which],
            recv_sem=recv_sem.at[which],
            device_id=device,
            device_id_type=MESH,
        )

    def send_e(o):
        send(e_send, e_recv.at[pl.ds(o - 1, 1)], 0, {"cl": partner(me, o, n_cl)}).start()

    for_others(n_cl, send_e)
    tile = bv.at[pl.ds((count - 1) * clusters, clusters)]
    halos = [
        pltpu.make_async_remote_copy(
            src_ref=tile,
            dst_ref=halo.at[i],
            send_sem=halo_sem.at[i],
            recv_sem=halo_sem.at[2 + i],
            device_id={"cl": rest(me + shift, n_cl)},
            device_id_type=MESH,
        )
        for i, shift in enumerate((1, n_cl - 1))
    ]
    for copy in halos:
        copy.start()

    def send_ga(o):
        send(ga_send, ga_recv.at[pl.ds(o - 1, 1)], 1, {"cl": partner(me, o, n_cl)}).start()

    for_others(n_cl, send_ga)

    def arrived(ref, which):
        pltpu.make_async_copy(ref, ref, recv_sem.at[which]).wait()

    def left(ref, which):
        pltpu.make_async_copy(ref, ref, send_sem.at[which]).wait()

    arrived(e_recv, 0)
    rows = jnp.concatenate([e_send[...], e_recv[...]], axis=0)
    rows = jnp.where(own_lane[None], jnp.broadcast_to(rows, (n_cl, clusters, wide)), 0.0)
    picked = dot(one_hot, rows.reshape(all_cl, wide).astype(bf16)).astype(bf16)
    product = dot(picked, spread[...]) * cv[...].astype(f32)
    high = product.astype(bf16)
    low = (product - high.astype(f32)).astype(bf16)
    both = dot(jnp.concatenate([high, low], axis=0), gather[...])
    term = both[:slots] + both[slots:]
    term = jnp.where(target_lane, term, 0.0)

    def partial_for(device):
        return jnp.sum(jnp.where(target_dev == device, term, 0.0), axis=0, keepdims=True)

    for i, o in enumerate(offsets):
        p_send[i] = partial_for(rest(me + o, n_cl))
    for i, o in enumerate(offsets):
        send(p_send.at[i], p_recv.at[i], 2, {"cl": rest(me + o, n_cl)}).start()
    own_partial = partial_for(me)

    for i in range(2):
        halos[i].wait_recv()
    loads[6].wait()
    before = jnp.where(me > 0, halo[0], 0.0)
    after = jnp.where(me < n_cl - 1, halo[1], 0.0)
    window = jnp.concatenate([before, current, after], axis=0).astype(bf16)
    reach = window.shape[0]
    turn = iota((clusters, clusters), 0) == iota((clusters, clusters), 1)
    listed = [
        jnp.sum(jnp.where(turn, lv[k : k + 1, :], 0), axis=1, keepdims=True) for k in range(near_k)
    ]
    gathered = jnp.concatenate(
        [
            dot(
                jnp.where(iota((clusters, reach), 1) == listed[k], 1.0, 0.0).astype(bf16), window
            ).astype(bf16)
            for k in range(near_k)
        ],
        axis=1,
    )
    loads[7].wait()
    image = 0.5 * current
    pair = 2
    row_id = iota((clusters, width), 0)
    for t in range(0, clusters, pair):
        blocks = jnp.concatenate(
            [
                jnp.concatenate([nv[(t + u) * near_k + k] for k in range(near_k)], axis=1)
                for u in range(pair)
            ],
            axis=0,
        )
        result = dot_t(gathered, blocks)
        for u in range(pair):
            image += jnp.where(row_id == t + u, result[:, u * width : (u + 1) * width], 0.0)

    arrived(ga_recv, 1)
    group_gram = ga_send[0] + jnp.sum(ga_recv[...], axis=0)
    gb_send[0] = group_gram

    def send_gb(o):
        send(gb_send, gb_recv.at[pl.ds(o - 1, 1)], 3, {"grp": partner(grp, o, n_grp)}).start()

    for_others(n_grp, send_gb)

    loads[8].wait()
    arrived(p_recv, 2)
    coupled = own_partial + jnp.sum(p_recv[...], axis=0)
    coupled = jnp.where(own_lane, jnp.broadcast_to(coupled, (clusters, wide)), 0.0).astype(bf16)
    image += dot(coupled, tbv[...])

    basis3 = bv[...].reshape(count, clusters, width)
    sums = jnp.sum(basis3 * image[None], axis=1)
    squares = jnp.sum(image * image, axis=0, keepdims=True)
    tail = jnp.where(iota((8, width), 0) == 0, squares, 0.0)
    stacked = jnp.concatenate([sums, tail, jnp.zeros((width - count - 8, width), f32)], axis=0)
    ones = jnp.ones((8, width), bf16)
    row = sum(dot_t(ones, part) for part in parts3(stacked))[0:1]
    r_send[0] = row

    def send_r(o):
        send(r_send, r_recv.at[pl.ds(o - 1, 1)], 4, far_device(o)).start()

    for_others(total, send_r)

    arrived(gb_recv, 3)
    whole_gram = gb_send[0] + jnp.sum(gb_recv[...], axis=0)
    narrow = jnp.where(
        rest(iota((flat_gram, width), 0), count) == iota((flat_gram, width), 1), 1.0, 0.0
    ).astype(bf16)
    gram_rows = jnp.where(gram_lane, jnp.broadcast_to(whole_gram, (count, flat_gram)), 0.0)
    gram_full = sum(dot(part, narrow) for part in parts3(gram_rows))

    arrived(r_recv, 4)
    inverse = 1.0 / float(total * clusters * width)
    mean = (r_send[0] + jnp.sum(r_recv[...], axis=0)) * inverse
    diagonal = iota((count, width), 0) == iota((count, width), 1)
    projection = jnp.sum(jnp.where(diagonal, mean, 0.0), axis=1, keepdims=True)
    applied = jnp.sum(gram_full * mean, axis=1, keepdims=True) * inverse
    lane = iota((1, width), 1)
    image_mean = jnp.sum(jnp.where(lane == count, mean, 0.0), axis=1, keepdims=True)
    change = jnp.sum(projection * (applied - 2.0 * projection), axis=0, keepdims=True)
    norm = jnp.sqrt(image_mean + change + 1e-06)
    spread_p = jnp.broadcast_to(projection, (count, width))
    remainder = image - jnp.sum(basis3 * spread_p[:, None, :], axis=0)
    out_ref[...] = remainder * (1.0 / norm)
    hess_ref[...] = jnp.where(lane == count, norm, mean)[:, : count + 1]

    for i in range(2):
        halos[i].wait_send()
    left(e_recv, 0)
    left(ga_recv, 1)
    left(p_recv, 2)
    left(gb_recv, 3)
    left(r_recv, 4)


def hand_out(vector, column, vector_h, column_h, sem):
    copies = [
        pltpu.make_async_copy(vector, vector_h, sem.at[0]),
        pltpu.make_async_copy(column, column_h, sem.at[1]),
    ]
    for copy in copies:
        copy.start()
    for copy in copies:
        copy.wait()


def on_device(n_cl, n_grp, basis, near_blocks, near_list, source_basis, target_basis, coupling, far_target, far_source, far_count):
    count, _, clusters, width = basis.shape
    near_k = near_blocks.shape[2]
    ranks = source_basis.shape[2]
    slots = coupling.shape[1]
    wide = clusters * ranks
    square = ranks * ranks
    total = n_cl * n_grp
    offsets = target_offsets(n_cl)
    args = (
        basis.reshape(count * clusters, width),
        near_blocks.reshape(clusters * near_k, width, width),
        near_list.reshape(clusters, near_k).T,
        source_basis.reshape(wide, width),
        target_basis.reshape(wide, width),
        coupling.reshape(slots, square),
        far_target,
        far_source,
        far_count,
    )
    f32, bf16 = jnp.float32, jnp.bfloat16
    order = (0, 1, 2, 3, 4, 5, 6, 7, 8)
    next_vector, hessenberg = pl.pallas_call(
        functools.partial(kernel, n_cl, n_grp, offsets),
        out_shape=(
            pltpu.VMEM((clusters, width), f32),
            pltpu.VMEM((1, count + 1), f32),
        ),
        in_specs=[pl.BlockSpec(memory_space=pl.ANY)] * len(args),
        out_specs=(pl.BlockSpec(memory_space=pltpu.VMEM), pl.BlockSpec(memory_space=pltpu.VMEM)),
        scratch_shapes=[pltpu.VMEM(args[i].shape, args[i].dtype) for i in order]
        + [
            pltpu.VMEM((wide, square), bf16),
            pltpu.VMEM((square, wide), bf16),
            pltpu.VMEM((1, 1, wide), f32),
            pltpu.VMEM((n_cl - 1, 1, wide), f32),
            pltpu.VMEM((2, clusters, width), f32),
            pltpu.VMEM((len(offsets), 1, wide), f32),
            pltpu.VMEM((len(offsets), 1, wide), f32),
            pltpu.VMEM((1, 1, count * count), f32),
            pltpu.VMEM((n_cl - 1, 1, count * count), f32),
            pltpu.VMEM((1, 1, count * count), f32),
            pltpu.VMEM((n_grp - 1, 1, count * count), f32),
            pltpu.VMEM((1, 1, width), f32),
            pltpu.VMEM((total - 1, 1, width), f32),
            pltpu.SemaphoreType.DMA((9,)),
            pltpu.SemaphoreType.DMA((4,)),
            pltpu.SemaphoreType.DMA((5,)),
            pltpu.SemaphoreType.DMA((5,)),
        ],
        compiler_params=pltpu.CompilerParams(collective_id=0, has_side_effects=True),
        name="arnoldi_step",
    )(*args)
    next_vector = pltpu.with_memory_space_constraint(next_vector, pltpu.VMEM)
    hessenberg = pltpu.with_memory_space_constraint(hessenberg, pltpu.VMEM)
    next_vector, hessenberg = pl.pallas_call(
        hand_out,
        out_shape=(
            jax.ShapeDtypeStruct((clusters, width), f32),
            jax.ShapeDtypeStruct((1, count + 1), f32),
        ),
        in_specs=[pl.BlockSpec(memory_space=pltpu.VMEM)] * 2,
        out_specs=(pl.BlockSpec(memory_space=pl.ANY), pl.BlockSpec(memory_space=pl.ANY)),
        scratch_shapes=[pltpu.SemaphoreType.DMA((2,))],
        name="hand_out",
    )(next_vector, hessenberg)
    return next_vector.reshape(1, clusters, width), hessenberg.reshape(count + 1)


def solution(mesh):
    placed = (
        P(None, "grp", "cl", None),
        P("grp", "cl", None, None, None),
        P("grp", "cl", None),
        P("grp", "cl", None, None),
        P("grp", "cl", None, None),
        P("grp", "cl", None),
        P("grp", None),
        P("grp", "cl"),
        P("grp", "cl"),
    )
    return jax.shard_map(
        functools.partial(on_device, mesh.shape["cl"], mesh.shape["grp"]),
        mesh=mesh,
        in_specs=placed,
        out_specs=(P("grp", "cl", None), P()),
        check_vma=False,
    )
```

```python
import functools

import jax
import jax.numpy as jnp
from jax import lax
from jax.experimental import pallas as pl
from jax.experimental.pallas import tpu as pltpu
from jax.sharding import PartitionSpec as P

MESH = pl.DeviceIdType.MESH
TARGET_REACH = 2


def target_offsets(n_cl):
    near = {o % n_cl for r in range(1, TARGET_REACH + 1) for o in (r, -r)}
    return sorted((near | {n_cl // 2}) - {0}, key=lambda o: -min(o, n_cl - o))


def iota(shape, dim):
    return lax.broadcasted_iota(jnp.int32, shape, dim)


def power_of_two(n):
    return n & (n - 1) == 0


def quot(x, n):
    return lax.shift_right_logical(x, n.bit_length() - 1) if power_of_two(n) else lax.div(x, n)


def rest(x, n):
    return x & (n - 1) if power_of_two(n) else lax.rem(x, n)


def partner(me, o, n):
    return me ^ o if power_of_two(n) else lax.rem(me + o, n)


def place_of(me, device, n):
    return me ^ device if power_of_two(n) else lax.rem(me - device + n, n)


def for_others(n, body):
    if n <= 64:
        for o in reversed(range(1, n)):
            body(o)
    else:
        pl.loop(1, n)(body)


def parts3(x):
    hi = x.astype(jnp.bfloat16)
    rest = x - hi.astype(jnp.float32)
    mid = rest.astype(jnp.bfloat16)
    lo = (rest - mid.astype(jnp.float32)).astype(jnp.bfloat16)
    return hi, mid, lo


def dot_t(a, b):
    return lax.dot_general(a, b, (((1,), (1,)), ((), ())), preferred_element_type=jnp.float32)


def dot(a, b):
    return jnp.dot(a, b, preferred_element_type=jnp.float32)


def kernel(
    n_cl,
    n_grp,
    offsets,
    basis_h,
    near_h,
    list_h,
    sb_h,
    tb_h,
    coup_h,
    ft_h,
    fs_h,
    fc_h,
    out_ref,
    hess_ref,
    bv,
    nv,
    lv,
    sbv,
    tbv,
    cv,
    ftv,
    fsv,
    fcv,
    spread,
    gather,
    e_send,
    e_recv,
    halo,
    p_send,
    p_recv,
    ga_send,
    ga_recv,
    gb_send,
    gb_recv,
    r_send,
    r_recv,
    local_sem,
    halo_sem,
    send_sem,
    recv_sem,
):
    f32, bf16 = jnp.float32, jnp.bfloat16
    me, grp = lax.axis_index("cl"), lax.axis_index("grp")
    total = n_cl * n_grp
    flat_me = me * n_grp + grp
    near_k, clusters = lv.shape
    width = bv.shape[1]
    count = bv.shape[0] // clusters
    slots = cv.shape[0]
    ranks = sbv.shape[0] // clusters
    wide = clusters * ranks
    all_cl = n_cl * clusters

    barrier = pltpu.get_barrier_semaphore()

    def far_device(o):
        flat = partner(flat_me, o, total)
        return {"cl": quot(flat, n_grp), "grp": rest(flat, n_grp)}

    def greet(axis, mine, n):
        def one(o):
            device = {axis: partner(mine, o, n)}
            pl.semaphore_signal(barrier, inc=1, device_id=device, device_id_type=MESH)

        for_others(n, one)

    greet("cl", me, n_cl)
    greet("grp", grp, n_grp)
    loads = [
        pltpu.make_async_copy(src, dst, local_sem.at[i])
        for i, (src, dst) in enumerate(
            [
                (basis_h, bv),
                (sb_h, sbv),
                (coup_h, cv),
                (ft_h, ftv),
                (fs_h, fsv),
                (fc_h, fcv),
                (list_h, lv),
                (near_h, nv),
                (tb_h, tbv),
            ]
        )
    ]
    for load in loads:
        load.start()

    loads[0].wait()
    loads[1].wait()
    current = bv[(count - 1) * clusters :, :]
    current_bf = current.astype(bf16)
    own_lane = iota((clusters, wide), 0) == quot(iota((clusters, wide), 1), ranks)
    e8 = jnp.where(own_lane, dot_t(current_bf, sbv[...]), 0.0)
    e_send[0] = jnp.sum(e8, axis=0, keepdims=True).astype(bf16).astype(f32)

    pl.semaphore_wait(barrier, n_cl + n_grp - 2)

    def send(src, dst, which, device):
        return pltpu.make_async_remote_copy(
            src_ref=src,
            dst_ref=dst,
            send_sem=send_sem.at[which],
            recv_sem=recv_sem.at[which],
            device_id=device,
            device_id_type=MESH,
        )

    def send_e(o):
        send(e_send, e_recv.at[pl.ds(o - 1, 1)], 0, {"cl": partner(me, o, n_cl)}).start()

    for_others(n_cl, send_e)
    tile = bv.at[pl.ds((count - 1) * clusters, clusters)]
    halos = [
        pltpu.make_async_remote_copy(
            src_ref=tile,
            dst_ref=halo.at[i],
            send_sem=halo_sem.at[i],
            recv_sem=halo_sem.at[2 + i],
            device_id={"cl": rest(me + shift, n_cl)},
            device_id_type=MESH,
        )
        for i, shift in enumerate((1, n_cl - 1))
    ]
    for copy in halos:
        copy.start()

    repeat = jnp.where(
        iota((ranks, ranks * ranks), 0) == rest(iota((ranks, ranks * ranks), 1), ranks), 1.0, 0.0
    ).astype(bf16)
    for at in range(0, wide, ranks):
        spread[at : at + ranks, :] = repeat
    lane_rank = rest(iota((ranks, wide), 1), ranks)
    for r in range(ranks):
        gather[r * ranks : (r + 1) * ranks, :] = jnp.where(lane_rank == r, 1.0, 0.0).astype(bf16)

    for load in loads[2:6]:
        load.wait()
    eye = iota((slots, slots), 0) == iota((slots, slots), 1)
    sources = jnp.sum(jnp.where(eye, fsv[...], 0), axis=1, keepdims=True)
    live = iota((slots, 1), 0) < fcv[...]
    behind = place_of(me, quot(sources, clusters), n_cl)
    picked_row = jnp.where(live, behind * clusters + rest(sources, clusters), -1)
    one_hot = jnp.where(iota((slots, all_cl), 1) == picked_row, 1.0, 0.0).astype(bf16)
    slot_shape = (slots, ftv.shape[1])
    mine = iota(slot_shape, 1) == iota(slot_shape, 0) + me * slots
    targets = jnp.sum(jnp.where(mine, ftv[...], 0), axis=1, keepdims=True)
    target_dev = quot(targets, clusters)
    target_lane = rest(targets, clusters) == quot(iota((slots, wide), 1), ranks)

    gram = jnp.zeros((count, count), f32)
    for t in range(clusters):
        rows = bv[pl.ds(t, count, stride=clusters), :]
        gram += lax.dot_general(
            rows, rows, (((1,), (1,)), ((), ())), precision=lax.Precision.HIGHEST, preferred_element_type=f32
        )
    flat_gram = count * count
    widen = jnp.where(
        iota((count, flat_gram), 0) == rest(iota((count, flat_gram), 1), count), 1.0, 0.0
    ).astype(bf16)
    gram_lane = iota((count, flat_gram), 0) == quot(iota((count, flat_gram), 1), count)
    gram_wide = sum(dot(part, widen) for part in parts3(gram))
    ga_send[0] = jnp.sum(jnp.where(gram_lane, gram_wide, 0.0), axis=0, keepdims=True)

    def send_ga(o):
        send(ga_send, ga_recv.at[pl.ds(o - 1, 1)], 1, {"cl": partner(me, o, n_cl)}).start()

    for_others(n_cl, send_ga)

    def arrived(ref, which):
        pltpu.make_async_copy(ref, ref, recv_sem.at[which]).wait()

    def left(ref, which):
        pltpu.make_async_copy(ref, ref, send_sem.at[which]).wait()

    arrived(e_recv, 0)
    rows = jnp.concatenate([e_send[...], e_recv[...]], axis=0)
    rows = jnp.where(own_lane[None], jnp.broadcast_to(rows, (n_cl, clusters, wide)), 0.0)
    picked = dot(one_hot, rows.reshape(all_cl, wide).astype(bf16)).astype(bf16)
    product = dot(picked, spread[...]) * cv[...].astype(f32)
    high = product.astype(bf16)
    low = (product - high.astype(f32)).astype(bf16)
    both = dot(jnp.concatenate([high, low], axis=0), gather[...])
    term = both[:slots] + both[slots:]
    term = jnp.where(target_lane, term, 0.0)

    def partial_for(device):
        return jnp.sum(jnp.where(target_dev == device, term, 0.0), axis=0, keepdims=True)

    for i, o in enumerate(offsets):
        p_send[i] = partial_for(rest(me + o, n_cl))
    for i, o in enumerate(offsets):
        send(p_send.at[i], p_recv.at[i], 2, {"cl": rest(me + o, n_cl)}).start()
    own_partial = partial_for(me)

    for i in range(2):
        halos[i].wait_recv()
    loads[6].wait()
    before = jnp.where(me > 0, halo[0], 0.0)
    after = jnp.where(me < n_cl - 1, halo[1], 0.0)
    window = jnp.concatenate([before, current, after], axis=0).astype(bf16)
    reach = window.shape[0]
    turn = iota((clusters, clusters), 0) == iota((clusters, clusters), 1)
    listed = [
        jnp.sum(jnp.where(turn, lv[k : k + 1, :], 0), axis=1, keepdims=True) for k in range(near_k)
    ]
    gathered = jnp.concatenate(
        [
            dot(
                jnp.where(iota((clusters, reach), 1) == listed[k], 1.0, 0.0).astype(bf16), window
            ).astype(bf16)
            for k in range(near_k)
        ],
        axis=1,
    )
    loads[7].wait()
    image = 0.5 * current
    pair = 2
    row_id = iota((clusters, width), 0)
    for t in range(0, clusters, pair):
        blocks = jnp.concatenate(
            [
                jnp.concatenate([nv[(t + u) * near_k + k] for k in range(near_k)], axis=1)
                for u in range(pair)
            ],
            axis=0,
        )
        result = dot_t(gathered, blocks)
        for u in range(pair):
            image += jnp.where(row_id == t + u, result[:, u * width : (u + 1) * width], 0.0)

    arrived(ga_recv, 1)
    group_gram = ga_send[0] + jnp.sum(ga_recv[...], axis=0)
    gb_send[0] = group_gram

    def send_gb(o):
        send(gb_send, gb_recv.at[pl.ds(o - 1, 1)], 3, {"grp": partner(grp, o, n_grp)}).start()

    for_others(n_grp, send_gb)

    loads[8].wait()
    arrived(p_recv, 2)
    coupled = own_partial + jnp.sum(p_recv[...], axis=0)
    coupled = jnp.where(own_lane, jnp.broadcast_to(coupled, (clusters, wide)), 0.0).astype(bf16)
    image += dot(coupled, tbv[...])

    basis3 = bv[...].reshape(count, clusters, width)
    sums = jnp.sum(basis3 * image[None], axis=1)
    squares = jnp.sum(image * image, axis=0, keepdims=True)
    tail = jnp.where(iota((8, width), 0) == 0, squares, 0.0)
    totals = jnp.sum(jnp.concatenate([sums, tail], axis=0), axis=1, keepdims=True)
    place = iota((count + 8, width), 0) == iota((count + 8, width), 1)
    r_send[0] = jnp.sum(jnp.where(place, totals, 0.0), axis=0, keepdims=True)

    def send_r(o):
        send(r_send, r_recv.at[pl.ds(o - 1, 1)], 4, far_device(o)).start()

    for_others(total, send_r)

    arrived(gb_recv, 3)
    whole_gram = gb_send[0] + jnp.sum(gb_recv[...], axis=0)
    narrow = jnp.where(
        rest(iota((flat_gram, width), 0), count) == iota((flat_gram, width), 1), 1.0, 0.0
    ).astype(bf16)
    gram_rows = jnp.where(gram_lane, jnp.broadcast_to(whole_gram, (count, flat_gram)), 0.0)
    gram_full = sum(dot(part, narrow) for part in parts3(gram_rows))

    arrived(r_recv, 4)
    inverse = 1.0 / float(total * clusters * width)
    mean = (r_send[0] + jnp.sum(r_recv[...], axis=0)) * inverse
    diagonal = iota((count, width), 0) == iota((count, width), 1)
    projection = jnp.sum(jnp.where(diagonal, mean, 0.0), axis=1, keepdims=True)
    applied = jnp.sum(gram_full * mean, axis=1, keepdims=True) * inverse
    lane = iota((1, width), 1)
    image_mean = jnp.sum(jnp.where(lane == count, mean, 0.0), axis=1, keepdims=True)
    change = jnp.sum(projection * (applied - 2.0 * projection), axis=0, keepdims=True)
    norm = jnp.sqrt(image_mean + change + 1e-06)
    spread_p = jnp.broadcast_to(projection, (count, width))
    remainder = image - jnp.sum(basis3 * spread_p[:, None, :], axis=0)
    out_ref[...] = remainder * (1.0 / norm)
    hess_ref[...] = jnp.where(lane == count, norm, mean)[:, : count + 1]

    for i in range(2):
        halos[i].wait_send()
    left(e_recv, 0)
    left(ga_recv, 1)
    left(p_recv, 2)
    left(gb_recv, 3)
    left(r_recv, 4)


def hand_out(vector, column, vector_h, column_h, sem):
    copies = [
        pltpu.make_async_copy(vector, vector_h, sem.at[0]),
        pltpu.make_async_copy(column, column_h, sem.at[1]),
    ]
    for copy in copies:
        copy.start()
    for copy in copies:
        copy.wait()


def on_device(n_cl, n_grp, basis, near_blocks, near_list, source_basis, target_basis, coupling, far_target, far_source, far_count):
    count, _, clusters, width = basis.shape
    near_k = near_blocks.shape[2]
    ranks = source_basis.shape[2]
    slots = coupling.shape[1]
    wide = clusters * ranks
    square = ranks * ranks
    total = n_cl * n_grp
    offsets = target_offsets(n_cl)
    args = (
        basis.reshape(count * clusters, width),
        near_blocks.reshape(clusters * near_k, width, width),
        near_list.reshape(clusters, near_k).T,
        source_basis.reshape(wide, width),
        target_basis.reshape(wide, width),
        coupling.reshape(slots, square),
        far_target,
        far_source,
        far_count,
    )
    f32, bf16 = jnp.float32, jnp.bfloat16
    order = (0, 1, 2, 3, 4, 5, 6, 7, 8)
    next_vector, hessenberg = pl.pallas_call(
        functools.partial(kernel, n_cl, n_grp, offsets),
        out_shape=(
            pltpu.VMEM((clusters, width), f32),
            pltpu.VMEM((1, count + 1), f32),
        ),
        in_specs=[pl.BlockSpec(memory_space=pl.ANY)] * len(args),
        out_specs=(pl.BlockSpec(memory_space=pltpu.VMEM), pl.BlockSpec(memory_space=pltpu.VMEM)),
        scratch_shapes=[pltpu.VMEM(args[i].shape, args[i].dtype) for i in order]
        + [
            pltpu.VMEM((wide, square), bf16),
            pltpu.VMEM((square, wide), bf16),
            pltpu.VMEM((1, 1, wide), f32),
            pltpu.VMEM((n_cl - 1, 1, wide), f32),
            pltpu.VMEM((2, clusters, width), f32),
            pltpu.VMEM((len(offsets), 1, wide), f32),
            pltpu.VMEM((len(offsets), 1, wide), f32),
            pltpu.VMEM((1, 1, count * count), f32),
            pltpu.VMEM((n_cl - 1, 1, count * count), f32),
            pltpu.VMEM((1, 1, count * count), f32),
            pltpu.VMEM((n_grp - 1, 1, count * count), f32),
            pltpu.VMEM((1, 1, width), f32),
            pltpu.VMEM((total - 1, 1, width), f32),
            pltpu.SemaphoreType.DMA((9,)),
            pltpu.SemaphoreType.DMA((4,)),
            pltpu.SemaphoreType.DMA((5,)),
            pltpu.SemaphoreType.DMA((5,)),
        ],
        compiler_params=pltpu.CompilerParams(collective_id=0, has_side_effects=True),
        name="arnoldi_step",
    )(*args)
    next_vector = pltpu.with_memory_space_constraint(next_vector, pltpu.VMEM)
    hessenberg = pltpu.with_memory_space_constraint(hessenberg, pltpu.VMEM)
    next_vector, hessenberg = pl.pallas_call(
        hand_out,
        out_shape=(
            jax.ShapeDtypeStruct((clusters, width), f32),
            jax.ShapeDtypeStruct((1, count + 1), f32),
        ),
        in_specs=[pl.BlockSpec(memory_space=pltpu.VMEM)] * 2,
        out_specs=(pl.BlockSpec(memory_space=pl.ANY), pl.BlockSpec(memory_space=pl.ANY)),
        scratch_shapes=[pltpu.SemaphoreType.DMA((2,))],
        name="hand_out",
    )(next_vector, hessenberg)
    return next_vector.reshape(1, clusters, width), hessenberg.reshape(count + 1)


def solution(mesh):
    placed = (
        P(None, "grp", "cl", None),
        P("grp", "cl", None, None, None),
        P("grp", "cl", None),
        P("grp", "cl", None, None),
        P("grp", "cl", None, None),
        P("grp", "cl", None),
        P("grp", None),
        P("grp", "cl"),
        P("grp", "cl"),
    )
    return jax.shard_map(
        functools.partial(on_device, mesh.shape["cl"], mesh.shape["grp"]),
        mesh=mesh,
        in_specs=placed,
        out_specs=(P("grp", "cl", None), P()),
        check_vma=False,
    )
```
